32 devices in a mesh: mem: 4 (over y, x), col: 8 (over z, core).
Axes of the slice: x: 2, y: 2, z: 4, core: 2. Of those that a mesh axis runs over, the one named last changes fastest.
Arguments:
- increment: float32 [8, 131072], P(None, 'col'), may hold values from -6 to 6
- ensemble: bfloat16 [64, 8, 131072], P('mem', None, 'col'), may hold values from -15 to 15
- climate: float32 [8, 131072], P(None, 'col'), may hold values from 0.5 to 2
- restrict_dest: int32 [2048, 1], replicated, may hold values from 0 to 7; in each aligned block of 256 rows (0 to 255, 256 to 511, ...) at most 64 rows name the same one
- restrict_local: int32 [2048], replicated, may hold values from 0 to 255
- restrict_weight: float32 [131072], P('col'), may hold values from 0.05 to 0.2
- conv_blocks: bfloat16 [16, 4, 128, 128], P('col'), may hold values from -0.25 to 0.25
- neighbours: int32 [16, 4], P('col'), may hold values from 0 to 15, as said below
- interp_dest: int32 [2048, 2], replicated, may hold values from 0 to 7, all different within a row; in each aligned block of 256 rows (0 to 255, 256 to 511, ...) at most 128 rows name the same one
- interp_local: int32 [2048, 2], replicated, may hold values from 0 to 255
- interp_weight: float32 [2, 131072], P(None, 'col'), may hold values from 0.2 to 1
Outputs:
- once_applied: float32 [8, 131072], P(None, 'col')
- twice_applied: float32 [8, 131072], P(None, 'col')
The draws below stay inside these ranges and needn't reach their ends.
Inputs may be any that keep to these rules, and one draw needn't show every extreme that they name: `restrict_dest`: in each aligned block of 256 rows (the tiles of one index of col) no device number appears in more than 64 rows. `interp_dest`: the two entries of a row differ. In each aligned block of 256 rows no device number appears in more than 128 rows. `neighbours`: the 4 entries of row b are distinct blocks among b - 2 to b + 2, taken modulo 16.
All inputs are finite; a program needn't handle non-finite values.
Results may differ from the reference program's by a relative error of at most 0.008.
Values may be sent and summed in bfloat16 or wider, within the bound.
No kernel may reach another device: no remote copies, remote signals or barrier semaphores. Data moves between devices by JAX's collectives and lax.ppermute only.
A program may use at most 128 MiB of HBM per device.

```python
import math
import jax
import jax.numpy as jnp
import numpy as np
from jax import lax

LEVELS = 8
TILE = 64
BLK_DEV = 2
NEIGH = 4
COARSE_DEV = 256
CBLK = 128
CAP = 64
MEMBERS = 64
FINE = 131072
COARSE = 2048
BLOCKS = 16
N_COL = 8


def draw_neighbours(key, part):
    choices_count = 2 * BLK_DEV + 1
    scores = jax.random.randint(key, (BLOCKS, choices_count), 0, 1 << 20) * choices_count + jnp.arange(choices_count, dtype=jnp.int32)[None, :]
    ordering = jnp.argsort(scores, axis=1, stable=True)[:, :NEIGH]
    offsets = ordering - BLK_DEV
    return ((jnp.arange(BLOCKS, dtype=jnp.int32)[:, None] + offsets) % BLOCKS).astype(jnp.int32)


def touch_ends(values, stream_key, low, top_value):
    spot = [jax.random.randint(jax.random.fold_in(stream_key, axis), (), 0, length) for axis, length in enumerate(values.shape)]
    main_axis = values.shape.index(max(values.shape))
    neighbour = spot[:main_axis] + [(spot[main_axis] + 1) % values.shape[main_axis]] + spot[main_axis + 1:]
    return values.at[tuple(spot)].set(low).at[tuple(neighbour)].set(top_value)


def shard_levels(key, extent, cuts, smallest, largest):
    def one(position, parts):
        steps = jax.random.uniform(jax.random.fold_in(jax.random.fold_in(key, 6), position), (parts,), jnp.float32, smallest / len(cuts), largest / len(cuts))
        return jnp.repeat(jnp.exp(steps), extent[position] // parts).reshape((-1,) + (1,) * (len(extent) - position - 1))

    level = one(*cuts[0])
    for cut in cuts[1:]:
        level = level * one(*cut)
    return level


def deal_out(own_key, own, number, rows, number_of, top, limit, skew):
    ranking = jax.random.permutation(own_key, number_of)
    crowded, ordinary = load_shares(number_of, rows * top, limit, skew, True), load_shares(number_of, rows * top, limit, skew, False)
    places = jnp.arange(number_of)

    def named(sizes, turn):
        used = int((sizes > 0).sum())
        fixed = max(1, used // 4)
        moved = fixed + (places - fixed + turn * (used - fixed)) % max(1, number_of - fixed)
        return jnp.zeros((number_of,), jnp.int32).at[ranking[jnp.where(places < fixed, places, moved)]].set(jnp.asarray(sizes, jnp.int32))

    sizes = jnp.where(number % 4 == 0, named(crowded, number // 4), named(ordinary, number - number // 4 - 1))
    mixed = jax.random.permutation(jax.random.fold_in(own, 3), number_of)
    giver, taker = mixed[0:number_of // 2 * 2:2], mixed[1:number_of // 2 * 2:2]
    room = jnp.minimum(sizes[giver] - 1, limit - sizes[taker]) // 2
    room = jnp.where((giver == ranking[0]) | (taker == ranking[0]) | (sizes[taker] == 0), 0, jnp.maximum(room, 0))
    moved = jax.random.randint(jax.random.fold_in(own, 4), (number_of // 2,), 0, 1 << 20) % (room + 1)
    sizes = sizes.at[giver].add(-moved).at[taker].add(moved)
    items = jnp.searchsorted(jnp.cumsum(sizes), jnp.arange(rows * top), side="right").astype(jnp.int32)
    listing = items.reshape(top, rows).T
    listing = listing[jax.random.permutation(jax.random.fold_in(own, 1), rows)]
    turn = jax.random.randint(jax.random.fold_in(own, 2), (rows, 1), 0, top)
    return jnp.take_along_axis(listing, (jnp.arange(top)[None, :] + turn) % top, axis=1)


def load_shares(count, total, most, skew, full):
    weights = [(1 << 20) // math.isqrt(rank ** skew) + 1 for rank in range(1, count + 1)]
    largest = most if full else min(most, max(-(-total // count), total * weights[0] // sum(weights)))
    least = 1 if total - largest >= count - 1 else 0
    given, rest = [largest] + [least] * (count - 1), total - largest - least * (count - 1)
    while rest > 0:
        candidates = [i for i in range(1, count) if given[i] < largest] or [i for i in range(1, count) if given[i] < most]
        mass, remaining = sum([weights[i] for i in candidates]), rest
        for i in candidates:
            extra = min(most - given[i], max(1, remaining * weights[i] // mass), rest)
            given[i] = given[i] + extra
            rest = rest - extra
    return np.array(given)


def scatter_about(own_key, shape, spread, limit, split=(), kind=jnp.bfloat16):
    gain = shard_levels(own_key, shape, split, -0.22, 0.18) if split else 1.0
    result = jax.random.normal(own_key, shape, jnp.float32) * spread * gain
    return jnp.minimum(jnp.maximum(result, -limit), limit).astype(kind)


def setup_inputs(seed: int = 0) -> dict:
    keys = jax.random.split(jax.random.key(seed), 12)
    increment = scatter_about(keys[0], (LEVELS, FINE), 1.0, 6.0, ((1, 8),), jnp.float32)
    ensemble = scatter_about(keys[1], (MEMBERS, LEVELS, FINE), 2.5, 15.0, ((0, 4), (2, 8)))
    climate = jnp.clip(jnp.exp(math.log(2.0) - 1.3862944 * jax.random.uniform(keys[2], (LEVELS, FINE), jnp.float32) ** shard_levels(keys[2], (LEVELS, FINE), ((1, 8),), -0.2, 0.2)), 0.5, 2.0)
    restrict_dest_keys = jax.random.split(jax.random.fold_in(keys[3], 1), COARSE // COARSE_DEV)
    restrict_dest_turns = jax.random.permutation(jax.random.fold_in(keys[3], 3), COARSE // COARSE_DEV)
    restrict_dest = jax.vmap(lambda own, number: deal_out(jax.random.fold_in(keys[3], 2), own, number, COARSE_DEV, N_COL, 1, CAP, 2))(restrict_dest_keys, restrict_dest_turns).reshape((COARSE, 1))
    restrict_local = touch_ends(jax.random.randint(keys[4], (COARSE,), 0, COARSE_DEV), jax.random.fold_in(keys[4], 1), 0, COARSE_DEV - 1).astype(jnp.int32)
    restrict_weight = jnp.clip(jnp.exp(math.log(0.2) - 1.3862944 * jax.random.uniform(keys[5], (FINE,), jnp.float32) ** shard_levels(keys[5], (FINE,), ((0, 8),), -0.2, 0.2)), 0.05, 0.2)
    conv_blocks = scatter_about(keys[6], (BLOCKS, NEIGH, CBLK, CBLK), (NEIGH * CBLK) ** -0.5, 0.25, ((0, 8),))
    neighbours = draw_neighbours(jax.random.fold_in(keys[11], 71), 0)
    interp_dest_keys = jax.random.split(jax.random.fold_in(keys[8], 1), COARSE // COARSE_DEV)
    interp_dest_turns = jax.random.permutation(jax.random.fold_in(keys[8], 3), COARSE // COARSE_DEV)
    interp_dest = jax.vmap(lambda own, number: deal_out(jax.random.fold_in(keys[8], 2), own, number, COARSE_DEV, N_COL, 2, 2 * CAP, 1))(interp_dest_keys, interp_dest_turns).reshape((COARSE, 2))
    interp_local = touch_ends(jax.random.randint(keys[9], (COARSE, 2), 0, COARSE_DEV), jax.random.fold_in(keys[9], 1), 0, COARSE_DEV - 1).astype(jnp.int32)
    interp_weight = jnp.clip(0.2 + 0.8 * jax.random.uniform(keys[10], (2, FINE), jnp.float32) ** shard_levels(keys[10], (2, FINE), ((1, 8),), -0.2, 0.2), 0.2, 1.0)
    return {"increment": increment, "ensemble": ensemble, "climate": climate, "restrict_dest": restrict_dest, "restrict_local": restrict_local, "restrict_weight": restrict_weight, "conv_blocks": conv_blocks, "neighbours": neighbours, "interp_dest": interp_dest, "interp_local": interp_local, "interp_weight": interp_weight}


def apply_once(state, ensemble, climate, restrict_dest, restrict_local, restrict_weight, conv_blocks, neighbours, interp_dest, interp_local, interp_weight):
    restrict_node = (restrict_dest[:, 0] * COARSE_DEV + restrict_local).astype(jnp.int32)
    interp_node = (interp_dest * COARSE_DEV + interp_local).astype(jnp.int32)
    weighted = state * restrict_weight[None, :]
    tile_weights = interp_weight.reshape(2, COARSE, TILE)
    conv_float = conv_blocks.astype(jnp.float32)

    def member_term(running, member):
        product = member.astype(jnp.float32) * weighted
        partial_value = jnp.sum(product.reshape(LEVELS, COARSE, TILE), axis=2)
        coarse = jax.ops.segment_sum(partial_value.T, restrict_node, num_segments=COARSE)
        coarse = coarse.astype(jnp.bfloat16).astype(jnp.float32)
        blocks = coarse.reshape(BLOCKS, CBLK, LEVELS)
        picked = blocks[neighbours]
        convolved = jnp.einsum("bkij,bkjl->bil", conv_float, picked, precision=lax.Precision.HIGHEST)
        node_values = convolved.reshape(COARSE, LEVELS).astype(jnp.bfloat16).astype(jnp.float32)
        values = node_values[interp_node]
        first_term = values[:, 0, :].T[:, :, None] * tile_weights[0][None, :, :]
        second_term = values[:, 1, :].T[:, :, None] * tile_weights[1][None, :, :]
        interp = (first_term + second_term).reshape(LEVELS, FINE)
        return running + member.astype(jnp.float32) * interp, None

    running, unused = lax.scan(member_term, jnp.zeros((LEVELS, FINE), jnp.float32), ensemble)
    return climate * state + running / (MEMBERS - 1)


def reference(increment, ensemble, climate, restrict_dest, restrict_local, restrict_weight, conv_blocks, neighbours, interp_dest, interp_local, interp_weight):
    once_applied = apply_once(increment, ensemble, climate, restrict_dest, restrict_local, restrict_weight, conv_blocks, neighbours, interp_dest, interp_local, interp_weight)
    twice_applied = apply_once(once_applied, ensemble, climate, restrict_dest, restrict_local, restrict_weight, conv_blocks, neighbours, interp_dest, interp_local, interp_weight)
    return once_applied, twice_applied
```

```python
import functools

import jax
import jax.numpy as jnp
from jax import lax
from jax.experimental import pallas as pl
from jax.experimental.pallas import tpu as pltpu
from jax.sharding import PartitionSpec as P

TILE = 64
LANES = 128
ROWS16 = 16
VMEM_BYTES = 48 * 1024 * 1024
HALF = jnp.bfloat16
FULL = jnp.float32


def swap(array, axis, mask):
    size = lax.axis_size(axis)
    return lax.ppermute(array, axis, [(i, i ^ mask) for i in range(size)])


def gather_slots(array):
    size = lax.axis_size("col")
    myself = lax.axis_index("col")
    if size == 8:
        same_core = [array] + [swap(array, "col", mask) for mask in (6, 4, 2)]
        other_core = [swap(piece, "col", 1) for piece in same_core]
        masks = jnp.array([0, 6, 4, 2, 1, 7, 5, 3], jnp.int32)
        return same_core + other_core, masks ^ myself
    stacked = lax.all_gather(array, "col")
    return [stacked[i] for i in range(size)], jnp.arange(size, dtype=jnp.int32)


def tile_indicator(tiles, columns):
    tile = lax.broadcasted_iota(jnp.int32, (tiles, columns), 0)
    column = lax.broadcasted_iota(jnp.int32, (tiles, columns), 1)
    return (column >= tile * TILE) & (column < tile * TILE + TILE)


def tile_sums(state, weight, ensemble_ref, partial_ref):
    members, levels, width = ensemble_ref.shape
    tiles = width // TILE
    weighted = state * weight
    product = ensemble_ref[...].astype(FULL) * weighted[None]
    product = product.reshape(members * levels, width).astype(HALF)
    indicator = jnp.where(tile_indicator(tiles, width), 1.0, 0.0).astype(HALF)
    partial_ref[...] = lax.dot_general(
        indicator, product, (((1,), (1,)), ((), ())), preferred_element_type=FULL
    ).astype(HALF)


def first_kernel(state_ref, weight_ref, ensemble_ref, partial_ref):
    tile_sums(state_ref[...], weight_ref[...], ensemble_ref, partial_ref)


def second_kernel(
    scale, state_ref, climate_ref, mine_ref, theirs_ref, weight_ref, ensemble_ref, state_out, partial_ref
):
    total = mine_ref[...].astype(FULL) + theirs_ref[...].astype(FULL)
    state = climate_ref[...] * state_ref[...] + total * scale
    state_out[...] = state
    tile_sums(state, weight_ref[...], ensemble_ref, partial_ref)


def params():
    return pltpu.CompilerParams(vmem_limit_bytes=VMEM_BYTES)


def column_sizes(ensemble):
    members, levels, fine = ensemble.shape
    width = min(fine, LANES // 4 * TILE)
    return members, levels, fine, width, fine // width


def run_first(state, weight, ensemble):
    members, levels, fine, width, steps = column_sizes(ensemble)
    tiles = width // TILE
    return pl.pallas_call(
        first_kernel,
        grid=(steps,),
        in_specs=[
            pl.BlockSpec((levels, width), lambda i: (0, i)),
            pl.BlockSpec((1, width), lambda i: (0, i)),
            pl.BlockSpec((members, levels, width), lambda i: (0, 0, i)),
        ],
        out_specs=pl.BlockSpec((tiles, members * levels), lambda i: (i, 0)),
        out_shape=jax.ShapeDtypeStruct((fine // TILE, members * levels), HALF),
        compiler_params=params(),
        name="tile_sums_first",
    )(state, weight, ensemble)


def run_second(scale, state, climate, mine, theirs, weight, ensemble):
    members, levels, fine, width, steps = column_sizes(ensemble)
    tiles = width // TILE
    row = pl.BlockSpec((levels, width), lambda i: (0, i))
    return pl.pallas_call(
        functools.partial(second_kernel, scale),
        grid=(steps,),
        in_specs=[
            row,
            row,
            row,
            row,
            pl.BlockSpec((1, width), lambda i: (0, i)),
            pl.BlockSpec((members, levels, width), lambda i: (0, 0, i)),
        ],
        out_specs=[row, pl.BlockSpec((tiles, members * levels), lambda i: (i, 0))],
        out_shape=[
            jax.ShapeDtypeStruct((levels, fine), FULL),
            jax.ShapeDtypeStruct((fine // TILE, members * levels), HALF),
        ],
        compiler_params=params(),
        name="tile_sums_second",
    )(state, climate, mine, theirs, weight, ensemble)


def matrix_kernel(slots, blocks, neigh, target_ref, tile_row_ref, tile_block_ref, *refs):
    conv_refs, matrix_ref = refs[:slots], refs[slots]
    pairs = target_ref.shape[0]
    size = LANES
    nodes = blocks * size
    target = target_ref[...]
    chosen = jnp.zeros((pairs, neigh * size), FULL)
    for s in range(slots):
        node = lax.broadcasted_iota(jnp.int32, (pairs, nodes), 1) + s * nodes
        pick = jnp.where(node == target, 1.0, 0.0).astype(HALF)
        rows = [
            jnp.concatenate(
                [conv_refs[s][pl.ds((b * neigh + k) * size, size), :] for k in range(neigh)], axis=1
            )
            for b in range(blocks)
        ]
        chosen = chosen + jnp.dot(pick, jnp.concatenate(rows, axis=0), preferred_element_type=FULL)
    chosen = chosen.astype(HALF)
    table = jnp.concatenate(
        [ref[pl.ds(blocks * neigh * size, ROWS16), :] for ref in conv_refs], axis=0
    )
    slot_of = target // nodes
    block_of = slot_of * ROWS16 + (target - slot_of * nodes) // size
    entry = lax.broadcasted_iota(jnp.int32, (pairs, slots * ROWS16), 1)
    near = jnp.dot(
        jnp.where(entry == block_of, 1.0, 0.0).astype(HALF), table, preferred_element_type=FULL
    )
    for s in range(slots):
        span = pl.ds(s * nodes, nodes)
        row = lax.broadcasted_iota(jnp.int32, (size, nodes), 0)
        place = jnp.where(row == tile_row_ref[:, span], 1.0, 0.0).astype(HALF)
        block = tile_block_ref[:, span].astype(FULL)
        value = jnp.zeros((pairs, nodes), FULL)
        for k in range(neigh):
            moved = jnp.dot(chosen[:, k * size : (k + 1) * size], place, preferred_element_type=FULL)
            value = jnp.where(near[:, k : k + 1] == block, moved, value)
        matrix_ref[:, span] = value.astype(HALF)


def run_matrix(target, tile_row, tile_block, conv_all, blocks, neigh):
    slots = len(conv_all)
    return pl.pallas_call(
        functools.partial(matrix_kernel, slots, blocks, neigh),
        in_specs=[pl.BlockSpec(memory_space=pltpu.VMEM)] * (3 + slots),
        out_specs=pl.BlockSpec(memory_space=pltpu.VMEM),
        out_shape=jax.ShapeDtypeStruct((target.shape[0], tile_row.shape[1]), HALF),
        compiler_params=params(),
        name="pair_matrix",
    )(target, tile_row, tile_block, *conv_all)


def spread_kernel(slots, matrix_ref, ensemble_ref, weight_ref, *refs):
    partial_refs, out_ref, values_ref = refs[:slots], refs[slots], refs[slots + 1]
    members, levels, width = ensemble_ref.shape
    tiles = width // TILE
    feature = members * levels

    @pl.when(pl.program_id(0) == 0)
    def _():
        span = partial_refs[0].shape[0]
        pairs = matrix_ref.shape[0]
        values = jnp.zeros((pairs, feature), FULL)
        for s in range(slots):
            values = values + jnp.dot(
                matrix_ref[:, s * span : (s + 1) * span],
                partial_refs[s][...],
                preferred_element_type=FULL,
            )
        values = values.T
        half = 2 * tiles
        lane = lax.broadcasted_iota(jnp.int32, (feature, 2 * half), 1)
        for i in range(pairs // half):
            two = values[:, i // 2 * 2 * half : (i // 2 + 1) * 2 * half]
            turned = pltpu.roll(two, half, 1)
            keep = (lane < half) if i % 2 == 0 else (lane >= half)
            values_ref[i] = jnp.where(keep, two, turned).astype(HALF)

    inside = tile_indicator(tiles, width)
    high = weight_ref[...].astype(HALF).astype(FULL)
    low = weight_ref[...] - high
    weights = jnp.concatenate(
        [
            jnp.where(inside, part[k : k + 1, :], 0.0).astype(HALF)
            for part in (high, low)
            for k in range(2)
        ],
        axis=0,
    )
    left = values_ref[pl.program_id(0)]
    piece = 4 * LANES
    for c in range(0, width, piece):
        field = jnp.dot(left, weights[:, c : c + piece], preferred_element_type=FULL)
        field = field.reshape(members, levels, piece)
        terms = ensemble_ref[:, :, c : c + piece].astype(FULL) * field
        out_ref[:, c : c + piece] = jnp.sum(terms, axis=0).astype(HALF)


def run_spread(matrix, ensemble, interp_weight, partial_all):
    members, levels, fine, width, steps = column_sizes(ensemble)
    slots = len(partial_all)
    feature = members * levels
    whole = pl.BlockSpec(memory_space=pltpu.VMEM)
    return pl.pallas_call(
        functools.partial(spread_kernel, slots),
        grid=(steps,),
        in_specs=[
            whole,
            pl.BlockSpec((members, levels, width), lambda i: (0, 0, i)),
            pl.BlockSpec((2, width), lambda i: (0, i)),
        ]
        + [whole] * slots,
        out_specs=pl.BlockSpec((levels, width), lambda i: (0, i)),
        out_shape=jax.ShapeDtypeStruct((levels, fine), HALF),
        scratch_shapes=[pltpu.VMEM((steps, feature, LANES), HALF)],
        compiler_params=params(),
        name="spread",
    )(matrix, ensemble, interp_weight, *partial_all)


def add_half(one, two):
    return (one.astype(FULL) + two.astype(FULL)).astype(HALF)


def member_sum(local):
    size = lax.axis_size("mem")
    masks = [1 << i for i in range(size.bit_length() - 1)]
    middle = local.shape[1] // 2
    halves = [local[:, :middle], local[:, middle:]]
    orders = [masks, masks[::-1]]
    for step in range(len(masks) - 1):
        moved = [swap(part, "mem", order[step]) for part, order in zip(halves, orders)]
        halves = [add_half(part, other) for part, other in zip(halves, moved)]
    moved = [swap(part, "mem", order[-1]) for part, order in zip(halves, orders)]
    return jnp.concatenate(halves, axis=1), jnp.concatenate(moved, axis=1)


def per_device(
    increment,
    ensemble,
    climate,
    restrict_dest,
    restrict_local,
    restrict_weight,
    conv_blocks,
    neighbours,
    interp_dest,
    interp_local,
    interp_weight,
):
    col_count = lax.axis_size("col")
    myself = lax.axis_index("col")
    members, levels, fine, width, steps = column_sizes(ensemble)
    coarse_local = fine // TILE
    blocks, neigh = neighbours.shape
    node_block = coarse_local // blocks
    scale = 1.0 / (members * lax.axis_size("mem") - 1)
    weight = restrict_weight[None, :]

    near = jnp.pad(
        neighbours.astype(HALF), ((0, ROWS16 - blocks), (0, node_block - neigh))
    )
    rows = conv_blocks.reshape(blocks * neigh * node_block, node_block)
    conv_all, sources = gather_slots(jnp.concatenate([rows, near], axis=0))

    owner = lax.dynamic_slice_in_dim(interp_dest, myself * coarse_local, coarse_local, 0)
    local = lax.dynamic_slice_in_dim(interp_local, myself * coarse_local, coarse_local, 0)
    slot = jnp.sum(
        jnp.where(owner[:, :, None] == sources[None, None, :], jnp.arange(col_count)[None, None, :], 0),
        axis=2,
    )
    target = slot * coarse_local + local
    target = target.reshape(steps, width // TILE, 2).transpose(0, 2, 1).reshape(-1, 1)
    owner_all = restrict_dest[:, 0].reshape(col_count, coarse_local)[sources].reshape(1, -1)
    local_all = restrict_local.reshape(col_count, coarse_local)[sources].reshape(1, -1)
    tile_row = local_all % node_block
    tile_block = owner_all * blocks + local_all // node_block

    partial = run_first(increment, weight, ensemble)
    partial_all, _ = gather_slots(partial)
    matrix = run_matrix(target, tile_row, tile_block, conv_all, blocks, neigh)
    mine, theirs = member_sum(run_spread(matrix, ensemble, interp_weight, partial_all))
    once_applied, partial = run_second(scale, increment, climate, mine, theirs, weight, ensemble)
    partial_all, _ = gather_slots(partial)
    mine, theirs = member_sum(run_spread(matrix, ensemble, interp_weight, partial_all))
    total = mine.astype(FULL) + theirs.astype(FULL)
    return once_applied, climate * once_applied + total * scale


def solution(mesh):
    in_specs = (
        P(None, "col"),
        P("mem", None, "col"),
        P(None, "col"),
        P(),
        P(),
        P("col"),
        P("col", None, None, None),
        P("col", None),
        P(),
        P(),
        P(None, "col"),
    )
    out_specs = (P(None, "col"), P(None, "col"))
    return jax.shard_map(
        per_device, mesh=mesh, in_specs=in_specs, out_specs=out_specs, check_vma=False
    )
```

```python
import functools

import jax
import jax.numpy as jnp
from jax import lax
from jax.experimental import pallas as pl
from jax.experimental.pallas import tpu as pltpu
from jax.sharding import PartitionSpec as P

TILE = 64
LANES = 128
VMEM_BYTES = 16 * 1024 * 1024
HALF = jnp.bfloat16
FULL = jnp.float32


def swap(array, axis, mask):
    size = lax.axis_size(axis)
    return lax.ppermute(array, axis, [(i, i ^ mask) for i in range(size)])


def gather_slots(array):
    size = lax.axis_size("col")
    myself = lax.axis_index("col")
    if size == 8:
        same_core = [array] + [swap(array, "col", mask) for mask in (6, 4, 2)]
        other_core = [swap(piece, "col", 1) for piece in same_core]
        masks = jnp.array([0, 6, 4, 2, 1, 7, 5, 3], jnp.int32)
        return same_core + other_core, masks ^ myself
    stacked = lax.all_gather(array, "col")
    return [stacked[i] for i in range(size)], jnp.arange(size, dtype=jnp.int32)


def tile_indicator(tiles, columns):
    tile = lax.broadcasted_iota(jnp.int32, (tiles, columns), 0)
    column = lax.broadcasted_iota(jnp.int32, (tiles, columns), 1)
    return (column >= tile * TILE) & (column < tile * TILE + TILE)


def ones_where(mask):
    return jnp.where(mask, 1.0, 0.0).astype(HALF)


def tile_sums(weighted, ensemble):
    members, levels, width = ensemble.shape
    product = ensemble.astype(FULL) * weighted[None]
    product = product.reshape(members * levels, width).astype(HALF)
    return lax.dot_general(
        ones_where(tile_indicator(width // TILE, width)),
        product,
        (((1,), (1,)), ((), ())),
        preferred_element_type=FULL,
    ).astype(HALF)


def whole(count):
    return [pl.BlockSpec(memory_space=pltpu.VMEM)] * count


def params():
    return pltpu.CompilerParams(vmem_limit_bytes=VMEM_BYTES)


def column_sizes(ensemble):
    members, levels, fine = ensemble.shape
    width = min(fine, LANES // 4 * TILE)
    return members, levels, fine, width, fine // width


def first_kernel(
    width, state_hbm, weight_hbm, ensemble_hbm, ensemble_ref, partial_ref, state_ref, weight_ref, sems
):
    fine = state_hbm.shape[1]
    tiles = width // TILE
    steps = fine // width
    copies = []
    for i in range(steps):
        span = pl.ds(i * width, width)
        copies.append(
            [
                pltpu.make_async_copy(source.at[:, span], target.at[:, span], sems.at[i, j])
                for j, (source, target) in enumerate(
                    [(state_hbm, state_ref), (weight_hbm, weight_ref)]
                )
            ]
            + [
                pltpu.make_async_copy(
                    ensemble_hbm.at[:, :, span], ensemble_ref.at[:, :, span], sems.at[i, 2]
                )
            ]
        )
    for group in copies:
        for copy in group:
            copy.start()
    for i, group in enumerate(copies):
        for copy in group:
            copy.wait()
        span = pl.ds(i * width, width)
        weighted = state_ref[:, span] * weight_ref[:, span]
        partial_ref[pl.ds(i * tiles, tiles), :] = tile_sums(weighted, ensemble_ref[:, :, span])


def run_first(state, weight, ensemble):
    members, levels, fine, width, steps = column_sizes(ensemble)
    return pl.pallas_call(
        functools.partial(first_kernel, width),
        in_specs=[pl.BlockSpec(memory_space=pltpu.HBM)] * 3,
        out_specs=whole(2),
        out_shape=[
            jax.ShapeDtypeStruct(ensemble.shape, ensemble.dtype),
            jax.ShapeDtypeStruct((fine // TILE, members * levels), HALF),
        ],
        scratch_shapes=[
            pltpu.VMEM((levels, fine), FULL),
            pltpu.VMEM((1, fine), FULL),
            pltpu.SemaphoreType.DMA((steps, 3)),
        ],
        compiler_params=params(),
        name="tile_sums_first",
    )(state, weight, ensemble)


def second_kernel(
    width,
    scale,
    state_ref,
    climate_ref,
    mine_ref,
    theirs_ref,
    weight_ref,
    ensemble_ref,
    state_out,
    partial_ref,
):
    tiles = width // TILE

    def step(i, carry):
        span = pl.ds(pl.multiple_of(i * width, width), width)
        total = mine_ref[:, span].astype(FULL) + theirs_ref[:, span].astype(FULL)
        state = climate_ref[:, span] * state_ref[:, span] + total * scale
        state_out[:, span] = state
        rows = pl.ds(pl.multiple_of(i * tiles, tiles), tiles)
        partial_ref[rows, :] = tile_sums(state * weight_ref[:, span], ensemble_ref[:, :, span])
        return carry

    lax.fori_loop(0, state_ref.shape[1] // width, step, 0)


def run_second(scale, state, climate, mine, theirs, weight, ensemble):
    members, levels, fine, width, steps = column_sizes(ensemble)
    return pl.pallas_call(
        functools.partial(second_kernel, width, scale),
        in_specs=whole(6),
        out_specs=whole(2),
        out_shape=[
            jax.ShapeDtypeStruct((levels, fine), FULL),
            jax.ShapeDtypeStruct((fine // TILE, members * levels), HALF),
        ],
        compiler_params=params(),
        name="tile_sums_second",
    )(state, climate, mine, theirs, weight, ensemble)


def tables_kernel(tile_node_ref, near_node_ref, target_ref, conv_ref, matrix_ref, select_ref):
    blocks, neigh, size, _ = conv_ref.shape
    nodes = blocks * size
    rows = [
        jnp.concatenate([conv_ref[b, k] for k in range(neigh)], axis=1) for b in range(blocks)
    ]

    def step(s, carry):
        span = pl.ds(pl.multiple_of(s * nodes, nodes), nodes)
        tile_node = tile_node_ref[:, span]
        for b in range(blocks):
            place = ones_where(near_node_ref[b] == tile_node)
            matrix_ref[pl.ds(b * size, size), span] = jnp.dot(
                rows[b], place, preferred_element_type=FULL
            ).astype(HALF)
        node = lax.broadcasted_iota(jnp.int32, (target_ref.shape[0], nodes), 1) + s * nodes
        select_ref[:, span] = ones_where(node == target_ref[...])
        return carry

    lax.fori_loop(0, tile_node_ref.shape[1] // nodes, step, 0)


def run_tables(tile_node, near_node, target, conv_blocks):
    blocks, neigh, size, _ = conv_blocks.shape
    total = tile_node.shape[1]
    return pl.pallas_call(
        tables_kernel,
        in_specs=whole(4),
        out_specs=whole(2),
        out_shape=[
            jax.ShapeDtypeStruct((blocks * size, total), HALF),
            jax.ShapeDtypeStruct((target.shape[0], total), HALF),
        ],
        compiler_params=params(),
        name="tables",
    )(tile_node, near_node, target, conv_blocks)


def slot_product(matrix_ref, piece_refs):
    span = piece_refs[0].shape[0]
    total = jnp.zeros((matrix_ref.shape[0], piece_refs[0].shape[1]), FULL)
    for s, piece in enumerate(piece_refs):
        total = total + jnp.dot(
            matrix_ref[:, s * span : (s + 1) * span], piece[...], preferred_element_type=FULL
        )
    return total


def nodes_kernel(matrix_ref, *refs):
    refs[-1][...] = slot_product(matrix_ref, refs[:-1]).astype(HALF)


def run_nodes(matrix, partial_all):
    return pl.pallas_call(
        nodes_kernel,
        in_specs=whole(1 + len(partial_all)),
        out_specs=whole(1)[0],
        out_shape=jax.ShapeDtypeStruct((matrix.shape[0], partial_all[0].shape[1]), HALF),
        compiler_params=params(),
        name="nodes",
    )(matrix, *partial_all)


def spread_kernel(width, slots, select_ref, ensemble_ref, weight_ref, *refs):
    node_refs, out_ref, values_ref = refs[:slots], refs[slots], refs[slots + 1]
    members, levels, fine = ensemble_ref.shape
    tiles = width // TILE
    feature = members * levels
    pairs = select_ref.shape[0]
    values = slot_product(select_ref, node_refs).T
    half = 2 * tiles
    lane = lax.broadcasted_iota(jnp.int32, (feature, 2 * half), 1)
    for i in range(pairs // half):
        two = values[:, i // 2 * 2 * half : (i // 2 + 1) * 2 * half]
        turned = pltpu.roll(two, half, 1)
        keep = (lane < half) if i % 2 == 0 else (lane >= half)
        values_ref[i] = jnp.where(keep, two, turned).astype(HALF)
    piece = 2 * LANES

    def step(i, carry):
        start = pl.multiple_of(i * width, width)
        inside = tile_indicator(tiles, width)
        weight = weight_ref[:, pl.ds(start, width)]
        high = weight.astype(HALF).astype(FULL)
        low = weight - high
        weights = jnp.concatenate(
            [
                jnp.where(inside, part[k : k + 1, :], 0.0).astype(HALF)
                for part in (high, low)
                for k in range(2)
            ],
            axis=0,
        )
        left = values_ref[i]
        for c in range(0, width, piece):
            field = jnp.dot(left, weights[:, c : c + piece], preferred_element_type=FULL)
            field = field.reshape(members, levels, piece)
            span = pl.ds(pl.multiple_of(start + c, piece), piece)
            terms = ensemble_ref[:, :, span].astype(FULL) * field
            out_ref[:, span] = jnp.sum(terms, axis=0).astype(HALF)
        return carry

    lax.fori_loop(0, fine // width, step, 0)


def run_spread(select, ensemble, interp_weight, nodes_all):
    members, levels, fine, width, steps = column_sizes(ensemble)
    slots = len(nodes_all)
    return pl.pallas_call(
        functools.partial(spread_kernel, width, slots),
        in_specs=whole(3 + slots),
        out_specs=whole(1)[0],
        out_shape=jax.ShapeDtypeStruct((levels, fine), HALF),
        scratch_shapes=[pltpu.VMEM((steps, members * levels, LANES), HALF)],
        compiler_params=params(),
        name="spread",
    )(select, ensemble, interp_weight, *nodes_all)


def add_half(one, two):
    return (one.astype(FULL) + two.astype(FULL)).astype(HALF)


def member_sum(local):
    size = lax.axis_size("mem")
    masks = [1 << i for i in range(size.bit_length() - 1)]
    middle = local.shape[1] // 2
    halves = [local[:, :middle], local[:, middle:]]
    orders = [masks, masks[::-1]]
    for step in range(len(masks) - 1):
        moved = [swap(part, "mem", order[step]) for part, order in zip(halves, orders)]
        halves = [add_half(part, other) for part, other in zip(halves, moved)]
    moved = [swap(part, "mem", order[-1]) for part, order in zip(halves, orders)]
    return jnp.concatenate(halves, axis=1), jnp.concatenate(moved, axis=1)


def per_device(
    increment,
    ensemble,
    climate,
    restrict_dest,
    restrict_local,
    restrict_weight,
    conv_blocks,
    neighbours,
    interp_dest,
    interp_local,
    interp_weight,
):
    col_count = lax.axis_size("col")
    myself = lax.axis_index("col")
    members, levels, fine, width, steps = column_sizes(ensemble)
    coarse_local = fine // TILE
    blocks, neigh = neighbours.shape
    node_block = coarse_local // blocks
    scale = 1.0 / (members * lax.axis_size("mem") - 1)
    weight = restrict_weight[None, :]

    ensemble, partial = run_first(increment, weight, ensemble)
    partial_all, sources = gather_slots(partial)

    owner = lax.dynamic_slice_in_dim(interp_dest, myself * coarse_local, coarse_local, 0)
    local = lax.dynamic_slice_in_dim(interp_local, myself * coarse_local, coarse_local, 0)
    slot = jnp.sum(
        jnp.where(owner[:, :, None] == sources[None, None, :], jnp.arange(col_count)[None, None, :], 0),
        axis=2,
    )
    target = slot * coarse_local + local
    target = target.reshape(steps, width // TILE, 2).transpose(0, 2, 1).reshape(-1, 1)
    node_all = restrict_dest[:, 0] * coarse_local + restrict_local
    tile_node = node_all.reshape(col_count, coarse_local)[sources].reshape(1, -1)
    near_node = neighbours[:, :, None] * node_block + jnp.arange(node_block, dtype=jnp.int32)
    near_node = near_node.reshape(blocks, neigh * node_block, 1)
    matrix, select = run_tables(tile_node, near_node, target, conv_blocks)

    nodes_all, _ = gather_slots(run_nodes(matrix, partial_all))
    mine, theirs = member_sum(run_spread(select, ensemble, interp_weight, nodes_all))
    once_applied, partial = run_second(scale, increment, climate, mine, theirs, weight, ensemble)
    partial_all, _ = gather_slots(partial)
    nodes_all, _ = gather_slots(run_nodes(matrix, partial_all))
    mine, theirs = member_sum(run_spread(select, ensemble, interp_weight, nodes_all))
    total = mine.astype(FULL) + theirs.astype(FULL)
    return once_applied, climate * once_applied + total * scale


def solution(mesh):
    in_specs = (
        P(None, "col"),
        P("mem", None, "col"),
        P(None, "col"),
        P(),
        P(),
        P("col"),
        P("col", None, None, None),
        P("col", None),
        P(),
        P(),
        P(None, "col"),
    )
    out_specs = (P(None, "col"), P(None, "col"))
    return jax.shard_map(
        per_device, mesh=mesh, in_specs=in_specs, out_specs=out_specs, check_vma=False
    )
```

```python
import functools

import jax
import jax.numpy as jnp
from jax import lax
from jax.experimental import pallas as pl
from jax.experimental.pallas import tpu as pltpu
from jax.sharding import PartitionSpec as P

TILE = 64
LANES = 128
FIRST_BYTES = 107 * 512 * 1024
VMEM_BYTES = 40 * 1024 * 1024
TABLE_BYTES = 32 * 1024 * 1024
HALF = jnp.bfloat16
FULL = jnp.float32


def swap(array, axis, mask):
    size = lax.axis_size(axis)
    return lax.ppermute(array, axis, [(i, i ^ mask) for i in range(size)])


def slot_masks():
    return (0, 2, 4, 6, 1, 3, 5, 7) if lax.axis_size("col") == 8 else None


def slot_source(masks, myself, slot):
    return slot if masks is None else myself ^ masks[slot]


def gather_slots(array):
    if slot_masks() is not None:
        same_core = [array] + [swap(array, "col", mask) for mask in (2, 4, 6)]
        return same_core + [swap(piece, "col", 1) for piece in same_core]
    stacked = lax.all_gather(array, "col")
    return [stacked[i] for i in range(lax.axis_size("col"))]


def tile_indicator(tiles, columns):
    tile = lax.broadcasted_iota(jnp.int32, (tiles, columns), 0)
    column = lax.broadcasted_iota(jnp.int32, (tiles, columns), 1)
    return (column >= tile * TILE) & (column < tile * TILE + TILE)


def ones_where(mask):
    return jnp.where(mask, 1.0, 0.0).astype(HALF)


def tile_sums(weighted, ensemble):
    members, levels, width = ensemble.shape
    product = ensemble.astype(FULL) * weighted[None]
    product = product.reshape(members * levels, width).astype(HALF)
    return lax.dot_general(
        ones_where(tile_indicator(width // TILE, width)),
        product,
        (((1,), (1,)), ((), ())),
        preferred_element_type=FULL,
    ).astype(HALF)


def whole(count):
    return [pl.BlockSpec(memory_space=pltpu.VMEM)] * count


def params(limit):
    return pltpu.CompilerParams(vmem_limit_bytes=limit)


def column_sizes(ensemble):
    members, levels, fine = ensemble.shape
    width = min(fine, LANES // 4 * TILE)
    return members, levels, fine, width, fine // width


def chunk_copy(source, target, sems, index, width, i):
    lead = (slice(None),) * (len(source.shape) - 1)
    span = pl.ds(pl.multiple_of(i * width, width), width)
    return pltpu.make_async_copy(
        source.at[lead + (span,)], target.at[lead + (span,)], sems.at[index, i]
    )


def first_kernel(
    width, state_hbm, weight_hbm, ensemble_hbm, partial_ref, state_ref, weight_ref, ensemble_ref, sems
):
    steps = state_hbm.shape[1] // width
    tiles = width // TILE
    pairs = [(state_hbm, state_ref), (weight_hbm, weight_ref), (ensemble_hbm, ensemble_ref)]

    def copies(i):
        return [
            chunk_copy(source, target, sems, j, width, i)
            for j, (source, target) in enumerate(pairs)
        ]

    for i in range(steps):
        for copy in copies(i):
            copy.start()

    def step(i, carry):
        for copy in copies(i):
            copy.wait()
        span = pl.ds(pl.multiple_of(i * width, width), width)
        weighted = state_ref[:, span] * weight_ref[:, span]
        rows = pl.ds(pl.multiple_of(i * tiles, tiles), tiles)
        partial_ref[rows, :] = tile_sums(weighted, ensemble_ref[:, :, span])
        return carry

    lax.fori_loop(0, steps, step, 0)


def run_first(state, weight, ensemble):
    members, levels, fine, width, steps = column_sizes(ensemble)
    return pl.pallas_call(
        functools.partial(first_kernel, width),
        in_specs=[pl.BlockSpec(memory_space=pltpu.HBM)] * 3,
        out_specs=whole(1)[0],
        out_shape=jax.ShapeDtypeStruct((fine // TILE, members * levels), HALF),
        scratch_shapes=[
            pltpu.VMEM((levels, fine), FULL),
            pltpu.VMEM((1, fine), FULL),
            pltpu.VMEM((members, levels, fine), HALF),
            pltpu.SemaphoreType.DMA((3, steps)),
        ],
        compiler_params=params(FIRST_BYTES),
        name="tile_sums_first",
    )(state, weight, ensemble)


def second_kernel(width, scale, ensemble_ref, state_ref, climate_ref, weight_ref, *refs):
    sum_refs, (state_out, partial_ref) = refs[:4], refs[4:]
    tiles = width // TILE
    half = sum_refs[0].shape[1] // width

    for part in range(2):
        mine_ref, theirs_ref = sum_refs[2 * part : 2 * part + 2]

        def step(j, carry):
            i = j + part * half
            span = pl.ds(pl.multiple_of(i * width, width), width)
            near = pl.ds(pl.multiple_of(j * width, width), width)
            total = mine_ref[:, near].astype(FULL) + theirs_ref[:, near].astype(FULL)
            state = climate_ref[:, span] * state_ref[:, span] + total * scale
            state_out[:, span] = state
            rows = pl.ds(pl.multiple_of(i * tiles, tiles), tiles)
            partial_ref[rows, :] = tile_sums(state * weight_ref[:, span], ensemble_ref[:, :, span])
            return carry

        lax.fori_loop(0, half, step, 0)


def run_second(scale, state, climate, sums, weight, ensemble):
    members, levels, fine, width, steps = column_sizes(ensemble)
    return pl.pallas_call(
        functools.partial(second_kernel, width, scale),
        in_specs=whole(8),
        out_specs=whole(2),
        out_shape=[
            jax.ShapeDtypeStruct((levels, fine), FULL),
            jax.ShapeDtypeStruct((fine // TILE, members * levels), HALF),
        ],
        compiler_params=params(VMEM_BYTES),
        name="tile_sums_second",
    )(ensemble, state, climate, weight, *sums)


def matrix_kernel(masks, myself_ref, near_ref, dest_ref, local_ref, conv_ref, matrix_ref):
    blocks, neigh, size, _ = conv_ref.shape
    nodes = blocks * size
    rows = [
        jnp.concatenate([conv_ref[b, k] for k in range(neigh)], axis=1) for b in range(blocks)
    ]
    row = lax.broadcasted_iota(jnp.int32, (size, nodes), 0)
    for s in range(dest_ref.shape[1] // nodes):
        source = slot_source(masks, myself_ref[0], s)
        span = pl.ds(pl.multiple_of(source * nodes, nodes), nodes)
        tile_node = dest_ref[:, span] * nodes + local_ref[:, span]
        for b in range(blocks):
            place = jnp.concatenate(
                [ones_where(row == tile_node - near_ref[b, k] * size) for k in range(neigh)], axis=0
            )
            matrix_ref[b * size : (b + 1) * size, s * nodes : (s + 1) * nodes] = jnp.dot(
                rows[b], place, preferred_element_type=FULL
            ).astype(HALF)


def run_matrix(myself, neighbours, dest, local, conv_blocks):
    blocks, neigh, size, _ = conv_blocks.shape
    scalars = pl.BlockSpec(memory_space=pltpu.SMEM)
    return pl.pallas_call(
        functools.partial(matrix_kernel, slot_masks()),
        in_specs=[scalars, scalars] + whole(3),
        out_specs=whole(1)[0],
        out_shape=jax.ShapeDtypeStruct((blocks * size, dest.shape[1]), HALF),
        compiler_params=params(TABLE_BYTES),
        name="node_matrix",
    )(myself, neighbours, dest, local, conv_blocks)


def select_kernel(masks, nodes, myself_ref, dest_ref, local_ref, select_ref):
    span = pl.ds(pl.multiple_of(myself_ref[0] * nodes, nodes), nodes)
    dest, local = (
        jnp.concatenate([ref[k : k + 1, span] for k in range(2)], axis=1)
        for ref in (dest_ref, local_ref)
    )
    row = lax.broadcasted_iota(jnp.int32, (nodes, 2 * nodes), 0)
    for s in range(dest_ref.shape[1] // nodes):
        source = slot_source(masks, myself_ref[0], s)
        select_ref[s * nodes : (s + 1) * nodes, :] = ones_where(
            row == jnp.where(dest == source, local, -1)
        )


def run_select(myself, dest, local, nodes):
    return pl.pallas_call(
        functools.partial(select_kernel, slot_masks(), nodes),
        in_specs=[pl.BlockSpec(memory_space=pltpu.SMEM)] + whole(2),
        out_specs=whole(1)[0],
        out_shape=jax.ShapeDtypeStruct((dest.shape[1], 2 * nodes), HALF),
        compiler_params=params(TABLE_BYTES),
        name="selection",
    )(myself, dest, local)


def nodes_kernel(matrix_ref, *refs):
    span = refs[0].shape[0]
    total = jnp.zeros(refs[-1].shape, FULL)
    for s, piece in enumerate(refs[:-1]):
        total = total + jnp.dot(
            matrix_ref[:, s * span : (s + 1) * span], piece[...], preferred_element_type=FULL
        )
    refs[-1][...] = total.astype(HALF)


def run_nodes(matrix, partial_all):
    return pl.pallas_call(
        nodes_kernel,
        in_specs=whole(1 + len(partial_all)),
        out_specs=whole(1)[0],
        out_shape=jax.ShapeDtypeStruct((matrix.shape[0], partial_all[0].shape[1]), HALF),
        compiler_params=params(TABLE_BYTES),
        name="nodes",
    )(matrix, *partial_all)


def spread_kernel(width, slots, ensemble_ref, select_ref, weight_ref, *refs):
    node_refs, out_refs, values_ref = refs[:slots], refs[slots : slots + 2], refs[slots + 2]
    members, levels, fine = ensemble_ref.shape
    tiles = width // TILE
    steps = fine // width
    feature = members * levels
    nodes = node_refs[0].shape[0]
    pairs = select_ref.shape[1]
    values = jnp.zeros((feature, pairs), FULL)
    for s, piece in enumerate(node_refs):
        values = values + lax.dot_general(
            piece[...],
            select_ref[s * nodes : (s + 1) * nodes, :],
            (((0,), (0,)), ((), ())),
            preferred_element_type=FULL,
        )
    lane = lax.broadcasted_iota(jnp.int32, (feature, LANES), 1)
    group = LANES // tiles
    for i in range(steps):
        first = i // group * LANES
        ends = [values[:, k * pairs // 2 + first : k * pairs // 2 + first + LANES] for k in range(2)]
        left = ends[0]
        for place in range(group):
            shift = (place - i % group) * tiles % LANES
            moved = ends[place % 2] if shift == 0 else pltpu.roll(ends[place % 2], shift, 1)
            left = moved if place == 0 else jnp.where(lane < place * tiles, left, moved)
        values_ref[i] = left.astype(HALF)
    piece = 2 * LANES

    for part in range(2):
        out_ref = out_refs[part]

        def step(j, carry):
            i = j + part * (steps // 2)
            inside = tile_indicator(tiles, width)
            weight = weight_ref[:, pl.ds(pl.multiple_of(i * width, width), width)]
            high = weight.astype(HALF).astype(FULL)
            low = weight - high
            weights = jnp.concatenate(
                [
                    jnp.where(inside, source[k : k + 1, :], 0.0).astype(HALF)
                    for source in (high, low)
                    for k in range(2)
                ],
                axis=0,
            )
            left = values_ref[i]
            for c in range(0, width, piece):
                field = jnp.dot(left, weights[:, c : c + piece], preferred_element_type=FULL)
                field = field.reshape(members, levels, piece)
                span = pl.ds(pl.multiple_of(i * width + c, piece), piece)
                terms = ensemble_ref[:, :, span].astype(FULL) * field
                near = pl.ds(pl.multiple_of(j * width + c, piece), piece)
                out_ref[:, near] = jnp.sum(terms, axis=0).astype(HALF)
            return carry

        lax.fori_loop(0, steps // 2, step, 0)


def run_spread(select, ensemble, interp_weight, nodes_all):
    members, levels, fine, width, steps = column_sizes(ensemble)
    slots = len(nodes_all)
    return pl.pallas_call(
        functools.partial(spread_kernel, width, slots),
        in_specs=whole(3 + slots),
        out_specs=whole(2),
        out_shape=[jax.ShapeDtypeStruct((levels, fine // 2), HALF)] * 2,
        scratch_shapes=[pltpu.VMEM((steps, members * levels, LANES), HALF)],
        compiler_params=params(VMEM_BYTES),
        name="spread",
    )(ensemble, select, interp_weight, *nodes_all)


def add_half(one, two):
    return (one.astype(FULL) + two.astype(FULL)).astype(HALF)


def member_sum(halves):
    size = lax.axis_size("mem")
    masks = [1 << i for i in range(size.bit_length() - 1)]
    orders = [masks, masks[::-1]]
    for step in range(len(masks) - 1):
        moved = [swap(part, "mem", order[step]) for part, order in zip(halves, orders)]
        halves = [add_half(part, other) for part, other in zip(halves, moved)]
    moved = [swap(part, "mem", order[-1]) for part, order in zip(halves, orders)]
    return halves[0], moved[0], halves[1], moved[1]


def per_device(
    increment,
    ensemble,
    climate,
    restrict_dest,
    restrict_local,
    restrict_weight,
    conv_blocks,
    neighbours,
    interp_dest,
    interp_local,
    interp_weight,
):
    myself = lax.axis_index("col")[None]
    members = ensemble.shape[0]
    nodes = ensemble.shape[2] // TILE
    scale = 1.0 / (members * lax.axis_size("mem") - 1)
    weight = restrict_weight[None, :]

    partial_all = gather_slots(run_first(increment, weight, ensemble))
    matrix = run_matrix(
        myself, neighbours, restrict_dest.reshape(1, -1), restrict_local.reshape(1, -1), conv_blocks
    )
    select = run_select(myself, interp_dest.T, interp_local.T, nodes)

    nodes_all = gather_slots(run_nodes(matrix, partial_all))
    sums = member_sum(run_spread(select, ensemble, interp_weight, nodes_all))
    once_applied, partial = run_second(scale, increment, climate, sums, weight, ensemble)
    nodes_all = gather_slots(run_nodes(matrix, gather_slots(partial)))
    sums = member_sum(run_spread(select, ensemble, interp_weight, nodes_all))
    total = jnp.concatenate(
        [sums[2 * i].astype(FULL) + sums[2 * i + 1].astype(FULL) for i in range(2)], axis=1
    )
    return once_applied, climate * once_applied + total * scale


def solution(mesh):
    in_specs = (
        P(None, "col"),
        P("mem", None, "col"),
        P(None, "col"),
        P(),
        P(),
        P("col"),
        P("col", None, None, None),
        P("col", None),
        P(),
        P(),
        P(None, "col"),
    )
    out_specs = (P(None, "col"), P(None, "col"))
    return jax.shard_map(
        per_device, mesh=mesh, in_specs=in_specs, out_specs=out_specs, check_vma=False
    )
```

```python
import functools

import jax
import jax.numpy as jnp
from jax import lax
from jax.experimental import pallas as pl
from jax.experimental.pallas import tpu as pltpu
from jax.sharding import PartitionSpec as P


TILE = 64
LANES = 128
FIRST_BYTES = 55040 * 1024
VMEM_BYTES = 40 * 1024 * 1024
TABLE_BYTES = 32 * 1024 * 1024
HALF = jnp.bfloat16
FULL = jnp.float32


def swap(array, axis, mask):
    size = lax.axis_size(axis)
    return lax.ppermute(array, axis, [(i, i ^ mask) for i in range(size)])


def slot_masks():
    return (0, 2, 4, 6, 1, 3, 5, 7) if lax.axis_size("col") == 8 else None


def slot_source(masks, myself, slot):
    return slot if masks is None else myself ^ masks[slot]


def gather_slots(array):
    if slot_masks() is not None:
        same_core = [array] + [swap(array, "col", mask) for mask in (2, 4, 6)]
        return same_core + [swap(p, "col", 1) for p in same_core]
    stacked = lax.all_gather(array, "col")
    return [stacked[i] for i in range(lax.axis_size("col"))]


def tile_indicator(tiles, columns):
    tile = lax.broadcasted_iota(jnp.int32, (tiles, columns), 0)
    column = lax.broadcasted_iota(jnp.int32, (tiles, columns), 1)
    return (column >= tile * TILE) & (column < tile * TILE + TILE)


def ones_where(mask):
    return jnp.where(mask, 1.0, 0.0).astype(HALF)


def tile_columns(width):
    tiles = width // TILE
    column = lax.broadcasted_iota(jnp.int32, (width, tiles), 0)
    tile = lax.broadcasted_iota(jnp.int32, (width, tiles), 1)
    return ones_where((column >= tile * TILE) & (column < tile * TILE + TILE))


def tile_sums(weighted, ensemble, columns):
    members, levels, width = ensemble.shape
    product = ensemble.astype(FULL) * weighted[None]
    product = product.reshape(members * levels, width).astype(HALF)
    return jnp.dot(product, columns, preferred_element_type=FULL)


def whole(count):
    return [pl.BlockSpec(memory_space=pltpu.VMEM)] * count


def params(limit):
    return pltpu.CompilerParams(vmem_limit_bytes=limit)


def column_sizes(ensemble):
    members, levels, fine = ensemble.shape
    width = min(fine, LANES // 4 * TILE)
    return members, levels, fine, width, fine // width


def chunk_copy(source, target, sems, index, width, i):
    lead = (slice(None),) * (len(source.shape) - 1)
    span = pl.ds(i * width, width)
    return pltpu.make_async_copy(
        source.at[lead + (span,)], target.at[lead + (span,)], sems.at[index, i]
    )


def first_kernel(
    width, state_hbm, weight_hbm, ensemble_hbm, partial_ref, state_ref, weight_ref, ensemble_ref, sems
):
    steps = state_hbm.shape[1] // width
    tiles = width // TILE
    pairs = [(state_hbm, state_ref), (weight_hbm, weight_ref), (ensemble_hbm, ensemble_ref)]

    def copies(i):
        return [
            chunk_copy(source, target, sems, j, width, i)
            for j, (source, target) in enumerate(pairs)
        ]

    for i in range(steps):
        for copy in copies(i):
            copy.start()
    columns = tile_columns(width)
    group = LANES // tiles
    for first in range(0, steps, group):
        sums = []
        for i in range(first, first + group):
            for copy in copies(i):
                copy.wait()
            span = slice(i * width, (i + 1) * width)
            weighted = state_ref[:, span] * weight_ref[:, span]
            sums.append(tile_sums(weighted, ensemble_ref[:, :, span], columns))
        place = slice(first * tiles, first * tiles + LANES)
        partial_ref[:, place] = jnp.concatenate(sums, axis=1).astype(HALF)


def run_first(state, weight, ensemble):
    members, levels, fine, width, steps = column_sizes(ensemble)
    return pl.pallas_call(
        functools.partial(first_kernel, width),
        in_specs=[pl.BlockSpec(memory_space=pltpu.HBM)] * 3,
        out_specs=whole(1)[0],
        out_shape=jax.ShapeDtypeStruct((members * levels, fine // TILE), HALF),
        scratch_shapes=[
            pltpu.VMEM((levels, fine), FULL),
            pltpu.VMEM((1, fine), FULL),
            pltpu.VMEM((members, levels, fine), HALF),
            pltpu.SemaphoreType.DMA((3, steps)),
        ],
        compiler_params=params(FIRST_BYTES),
        name="tile_sums_first",
    )(state, weight, ensemble)


def second_kernel(width, scale, columns_ref, ensemble_ref, state_ref, climate_ref, weight_ref, *refs):
    sum_refs, (state_out, partial_ref) = refs[:4], refs[4:]
    tiles = width // TILE
    steps = state_ref.shape[1] // width
    half = sum_refs[0].shape[1] // width
    group = LANES // tiles
    for first in range(0, steps, group):
        sums = []
        for i in range(first, first + group):
            mine_ref, theirs_ref = sum_refs[i // half * 2 : i // half * 2 + 2]
            span = slice(i * width, (i + 1) * width)
            near = slice(i % half * width, (i % half + 1) * width)
            total = mine_ref[:, near].astype(FULL) + theirs_ref[:, near].astype(FULL)
            state = climate_ref[:, span] * state_ref[:, span] + total * scale
            state_out[:, span] = state
            sums.append(tile_sums(state * weight_ref[:, span], ensemble_ref[:, :, span], columns_ref[...]))
        place = slice(first * tiles, first * tiles + LANES)
        partial_ref[:, place] = jnp.concatenate(sums, axis=1).astype(HALF)


def run_second(scale, columns, state, climate, sums, weight, ensemble):
    members, levels, fine, width, _ = column_sizes(ensemble)
    return pl.pallas_call(
        functools.partial(second_kernel, width, scale),
        in_specs=whole(9),
        out_specs=whole(2),
        out_shape=[
            jax.ShapeDtypeStruct((levels, fine), FULL),
            jax.ShapeDtypeStruct((members * levels, fine // TILE), HALF),
        ],
        compiler_params=params(VMEM_BYTES),
        name="tile_sums_second",
    )(columns, ensemble, state, climate, weight, *sums)


def matrix_kernel(masks, myself_ref, near_ref, dest_ref, local_ref, conv_ref, matrix_ref):
    blocks, neigh, size, _ = conv_ref.shape
    nodes = blocks * size
    rows = [
        jnp.concatenate([conv_ref[b, k] for k in range(neigh)], axis=1) for b in range(blocks)
    ]
    row = lax.broadcasted_iota(jnp.int32, (size, nodes), 0)
    for s in range(dest_ref.shape[1] // nodes):
        source = slot_source(masks, myself_ref[0], s)
        span = pl.ds(pl.multiple_of(source * nodes, nodes), nodes)
        tile_node = dest_ref[:, span] * nodes + local_ref[:, span]
        for b in range(blocks):
            place = jnp.concatenate(
                [ones_where(row == tile_node - near_ref[b, k] * size) for k in range(neigh)], axis=0
            )
            block = jnp.dot(rows[b], place, preferred_element_type=FULL)
            matrix_ref[s * nodes : (s + 1) * nodes, b * size : (b + 1) * size] = block.T.astype(HALF)


def run_matrix(myself, neighbours, dest, local, conv_blocks):
    blocks, _, size, _ = conv_blocks.shape
    scalars = pl.BlockSpec(memory_space=pltpu.SMEM)
    return pl.pallas_call(
        functools.partial(matrix_kernel, slot_masks()),
        in_specs=[scalars, scalars] + whole(3),
        out_specs=whole(1)[0],
        out_shape=jax.ShapeDtypeStruct((dest.shape[1], blocks * size), HALF),
        compiler_params=params(TABLE_BYTES),
        name="node_matrix",
    )(myself, neighbours, dest, local, conv_blocks)


def select_kernel(masks, nodes, myself_ref, dest_ref, local_ref, select_ref):
    span = pl.ds(pl.multiple_of(myself_ref[0] * nodes, nodes), nodes)
    dest, local = (
        jnp.concatenate([ref[k : k + 1, span] for k in range(2)], axis=1)
        for ref in (dest_ref, local_ref)
    )
    row = lax.broadcasted_iota(jnp.int32, (nodes, 2 * nodes), 0)
    for s in range(dest_ref.shape[1] // nodes):
        source = slot_source(masks, myself_ref[0], s)
        select_ref[s * nodes : (s + 1) * nodes, :] = ones_where(
            row == jnp.where(dest == source, local, -1)
        )


def run_select(myself, dest, local, nodes):
    return pl.pallas_call(
        functools.partial(select_kernel, slot_masks(), nodes),
        in_specs=[pl.BlockSpec(memory_space=pltpu.SMEM)] + whole(2),
        out_specs=whole(1)[0],
        out_shape=jax.ShapeDtypeStruct((dest.shape[1], 2 * nodes), HALF),
        compiler_params=params(TABLE_BYTES),
        name="selection",
    )(myself, dest, local)


def slot_product(piece_refs, matrix_ref):
    span = piece_refs[0].shape[1]
    total = jnp.zeros((piece_refs[0].shape[0], matrix_ref.shape[1]), FULL)
    for s, piece in enumerate(piece_refs):
        total = total + jnp.dot(
            piece[...], matrix_ref[s * span : (s + 1) * span, :], preferred_element_type=FULL
        )
    return total


def nodes_kernel(matrix_ref, *refs):
    refs[-1][...] = slot_product(refs[:-1], matrix_ref).astype(HALF)


def run_nodes(matrix, partial_all):
    return pl.pallas_call(
        nodes_kernel,
        in_specs=whole(1 + len(partial_all)),
        out_specs=whole(1)[0],
        out_shape=jax.ShapeDtypeStruct((partial_all[0].shape[0], matrix.shape[1]), HALF),
        compiler_params=params(TABLE_BYTES),
        name="nodes",
    )(matrix, *partial_all)


def expansion_kernel(width, weight_ref, expand_ref, columns_ref):
    columns_ref[...] = tile_columns(width)
    inside = tile_indicator(width // TILE, width)

    def step(i, carry):
        weight = weight_ref[:, pl.ds(pl.multiple_of(i * width, width), width)]
        high = weight.astype(HALF).astype(FULL)
        low = weight - high
        expand_ref[i] = jnp.concatenate(
            [
                jnp.where(inside, source[k : k + 1, :], 0.0).astype(HALF)
                for source in (high, low)
                for k in range(2)
            ],
            axis=0,
        )
        return carry

    lax.fori_loop(0, expand_ref.shape[0], step, 0)


def run_expansion(width, interp_weight):
    return pl.pallas_call(
        functools.partial(expansion_kernel, width),
        in_specs=whole(1),
        out_specs=whole(2),
        out_shape=[
            jax.ShapeDtypeStruct((interp_weight.shape[1] // width, 4 * width // TILE, width), HALF),
            jax.ShapeDtypeStruct((width, width // TILE), HALF),
        ],
        compiler_params=params(TABLE_BYTES),
        name="expansion",
    )(interp_weight)


def spread_kernel(slots, ensemble_ref, select_ref, expand_ref, *refs):
    node_refs, out_refs, values_ref = refs[:slots], refs[slots : slots + 2], refs[slots + 2]
    members, levels, _ = ensemble_ref.shape
    steps, _, width = expand_ref.shape
    tiles = width // TILE
    feature = members * levels
    pairs = select_ref.shape[1]
    values = slot_product(node_refs, select_ref)
    lane = lax.broadcasted_iota(jnp.int32, (feature, LANES), 1)
    group = LANES // tiles
    for i in range(steps):
        first = i // group * LANES
        ends = [values[:, k * pairs // 2 + first : k * pairs // 2 + first + LANES] for k in range(2)]
        left = ends[0]
        for place in range(group):
            shift = (place - i % group) * tiles % LANES
            moved = ends[place % 2] if shift == 0 else pltpu.roll(ends[place % 2], shift, 1)
            left = moved if place == 0 else jnp.where(lane < place * tiles, left, moved)
        values_ref[i] = left.astype(HALF)
    piece = 2 * LANES

    half = steps // 2
    for i in range(steps):
        for c in range(0, width, piece):
            field = jnp.dot(
                values_ref[i], expand_ref[i, :, c : c + piece], preferred_element_type=FULL
            )
            field = field.reshape(members, levels, piece)
            start = i * width + c
            terms = ensemble_ref[:, :, start : start + piece].astype(FULL) * field
            start = i % half * width + c
            out_refs[i // half][:, start : start + piece] = jnp.sum(terms, axis=0).astype(HALF)


def run_spread(select, ensemble, expand, nodes_all):
    members, levels, fine, _, steps = column_sizes(ensemble)
    slots = len(nodes_all)
    return pl.pallas_call(
        functools.partial(spread_kernel, slots),
        in_specs=whole(3 + slots),
        out_specs=whole(2),
        out_shape=[jax.ShapeDtypeStruct((levels, fine // 2), HALF)] * 2,
        scratch_shapes=[pltpu.VMEM((steps, members * levels, LANES), HALF)],
        compiler_params=params(VMEM_BYTES),
        name="spread",
    )(ensemble, select, expand, *nodes_all)


def add_half(one, two):
    return (one.astype(FULL) + two.astype(FULL)).astype(HALF)


def member_sum(halves):
    size = lax.axis_size("mem")
    masks = [1 << i for i in range(size.bit_length() - 1)]
    orders = [masks, masks[::-1]]
    for step in range(len(masks) - 1):
        moved = [swap(part, "mem", order[step]) for part, order in zip(halves, orders)]
        halves = [add_half(part, other) for part, other in zip(halves, moved)]
    moved = [swap(part, "mem", order[-1]) for part, order in zip(halves, orders)]
    return halves[0], moved[0], halves[1], moved[1]


def per_device(
    increment,
    ensemble,
    climate,
    restrict_dest,
    restrict_local,
    restrict_weight,
    conv_blocks,
    neighbours,
    interp_dest,
    interp_local,
    interp_weight,
):
    myself = lax.axis_index("col")[None]
    members = ensemble.shape[0]
    nodes = ensemble.shape[2] // TILE
    scale = 1.0 / (members * lax.axis_size("mem") - 1)
    weight = restrict_weight[None, :]

    partial_all = gather_slots(run_first(increment, weight, ensemble))
    matrix = run_matrix(
        myself, neighbours, restrict_dest.reshape(1, -1), restrict_local.reshape(1, -1), conv_blocks
    )
    select = run_select(myself, interp_dest.T, interp_local.T, nodes)
    expand, columns = run_expansion(column_sizes(ensemble)[3], interp_weight)

    nodes_all = gather_slots(run_nodes(matrix, partial_all))
    sums = member_sum(run_spread(select, ensemble, expand, nodes_all))
    once_applied, partial = run_second(scale, columns, increment, climate, sums, weight, ensemble)
    nodes_all = gather_slots(run_nodes(matrix, gather_slots(partial)))
    sums = member_sum(run_spread(select, ensemble, expand, nodes_all))
    total = jnp.concatenate(
        [sums[2 * i].astype(FULL) + sums[2 * i + 1].astype(FULL) for i in range(2)], axis=1
    )
    return once_applied, climate * once_applied + total * scale


def solution(mesh):
    in_specs = (
        P(None, "col"),
        P("mem", None, "col"),
        P(None, "col"),
        P(),
        P(),
        P("col"),
        P("col", None, None, None),
        P("col", None),
        P(),
        P(),
        P(None, "col"),
    )
    out_specs = (P(None, "col"), P(None, "col"))

    return jax.shard_map(per_device, mesh=mesh, in_specs=in_specs, out_specs=out_specs, check_vma=False)
```

```python
import functools

import jax
import jax.numpy as jnp
from jax import lax
from jax.experimental import pallas as pl
from jax.experimental.pallas import tpu as pltpu
from jax.sharding import PartitionSpec as P


TILE = 64
EXTRA = 16
PAIR = 4
LANES = 128
FIRST_BYTES = 55136 * 1024
VMEM_BYTES = 40 * 1024 * 1024
TABLE_BYTES = 32 * 1024 * 1024
HALF = jnp.bfloat16
FULL = jnp.float32


def swap(array, axis, mask):
    size = lax.axis_size(axis)
    return lax.ppermute(array, axis, [(i, i ^ mask) for i in range(size)])


def is_paired():
    return lax.axis_size("col") == 8


def slot_source(masks, myself, slot):
    return slot if masks is None else myself ^ masks[slot]


def tile_masks():
    return (0, 2, 4, 6, 1, 3, 5, 7) if is_paired() else None


def node_masks():
    return (0, 4, 2, 6, 1, 5, 3, 7) if is_paired() else None


def gather_all(array):
    stacked = lax.all_gather(array, "col")
    return [stacked[i] for i in range(lax.axis_size("col"))]


def gather_tiles(array):
    if not is_paired():
        return gather_all(array)
    same_core = [array] + [swap(array, "col", mask) for mask in (2, 4, 6)]
    return same_core + [swap(p, "col", 1) for p in same_core]


def gather_nodes(array):
    if not is_paired():
        return gather_all(array)
    same_core = [array] + [swap(array, "col", mask) for mask in (4, 2, 6)]
    return same_core + [swap(p, "col", 1) for p in same_core]


def gather_pairs(array):
    same_core = [array, swap(array, "col", 2)]
    return same_core + [swap(p, "col", 1) for p in same_core]


def tile_indicator(tiles, columns):
    tile = lax.broadcasted_iota(jnp.int32, (tiles, columns), 0)
    column = lax.broadcasted_iota(jnp.int32, (tiles, columns), 1)
    return (column >= tile * TILE) & (column < tile * TILE + TILE)


def ones_where(mask):
    return jnp.where(mask, 1.0, 0.0).astype(HALF)


def tile_columns(width):
    tiles = width // TILE
    column = lax.broadcasted_iota(jnp.int32, (width, tiles), 0)
    tile = lax.broadcasted_iota(jnp.int32, (width, tiles), 1)
    return ones_where((column >= tile * TILE) & (column < tile * TILE + TILE))


def tile_sums(weighted, ensemble, columns):
    members, levels, width = ensemble.shape
    product = ensemble.astype(FULL) * weighted[None]
    product = product.reshape(members * levels, width).astype(HALF)
    return jnp.dot(product, columns, preferred_element_type=FULL)


def whole(count):
    return [pl.BlockSpec(memory_space=pltpu.VMEM)] * count


def params(limit):
    return pltpu.CompilerParams(vmem_limit_bytes=limit)


def column_sizes(ensemble):
    members, levels, fine = ensemble.shape
    width = min(fine, LANES // 4 * TILE)
    return members, levels, fine, width, fine // width


def chunk_copy(source, target, sems, index, width, i):
    lead = (slice(None),) * (len(source.shape) - 1)
    span = pl.ds(i * width, width)
    return pltpu.make_async_copy(
        source.at[lead + (span,)], target.at[lead + (span,)], sems.at[index, i]
    )


def first_kernel(
    width, state_hbm, weight_hbm, ensemble_hbm, partial_ref, state_ref, weight_ref, ensemble_ref, sems
):
    steps = state_hbm.shape[1] // width
    tiles = width // TILE
    pairs = [(state_hbm, state_ref), (weight_hbm, weight_ref), (ensemble_hbm, ensemble_ref)]

    def copies(i):
        return [
            chunk_copy(source, target, sems, j, width, i)
            for j, (source, target) in enumerate(pairs)
        ]

    for i in range(steps):
        for copy in copies(i):
            copy.start()
    columns = tile_columns(width)
    group = LANES // tiles
    for first in range(0, steps, group):
        sums = []
        for i in range(first, first + group):
            for copy in copies(i):
                copy.wait()
            span = slice(i * width, (i + 1) * width)
            weighted = state_ref[:, span] * weight_ref[:, span]
            sums.append(tile_sums(weighted, ensemble_ref[:, :, span], columns))
        place = slice(first * tiles, first * tiles + LANES)
        partial_ref[:, place] = jnp.concatenate(sums, axis=1).astype(HALF)


def run_first(state, weight, ensemble):
    members, levels, fine, width, steps = column_sizes(ensemble)
    return pl.pallas_call(
        functools.partial(first_kernel, width),
        in_specs=[pl.BlockSpec(memory_space=pltpu.HBM)] * 3,
        out_specs=whole(1)[0],
        out_shape=jax.ShapeDtypeStruct((members * levels, fine // TILE), HALF),
        scratch_shapes=[
            pltpu.VMEM((levels, fine), FULL),
            pltpu.VMEM((1, fine), FULL),
            pltpu.VMEM((members, levels, fine), HALF),
            pltpu.SemaphoreType.DMA((3, steps)),
        ],
        compiler_params=params(FIRST_BYTES),
        name="tile_sums_first",
    )(state, weight, ensemble)


def second_kernel(width, scale, columns_ref, ensemble_ref, state_ref, climate_ref, weight_ref, *refs):
    sum_refs, (state_out, partial_ref) = refs[:4], refs[4:]
    tiles = width // TILE
    steps = state_ref.shape[1] // width
    half = sum_refs[0].shape[1] // width
    group = LANES // tiles
    for first in range(0, steps, group):
        sums = []
        for i in range(first, first + group):
            mine_ref, theirs_ref = sum_refs[i // half * 2 : i // half * 2 + 2]
            span = slice(i * width, (i + 1) * width)
            near = slice(i % half * width, (i % half + 1) * width)
            total = mine_ref[:, near].astype(FULL) + theirs_ref[:, near].astype(FULL)
            state = climate_ref[:, span] * state_ref[:, span] + total * scale
            state_out[:, span] = state
            sums.append(tile_sums(state * weight_ref[:, span], ensemble_ref[:, :, span], columns_ref[...]))
        place = slice(first * tiles, first * tiles + LANES)
        partial_ref[:, place] = jnp.concatenate(sums, axis=1).astype(HALF)


def run_second(scale, columns, state, climate, sums, weight, ensemble):
    members, levels, fine, width, _ = column_sizes(ensemble)
    return pl.pallas_call(
        functools.partial(second_kernel, width, scale),
        in_specs=whole(9),
        out_specs=whole(2),
        out_shape=[
            jax.ShapeDtypeStruct((levels, fine), FULL),
            jax.ShapeDtypeStruct((members * levels, fine // TILE), HALF),
        ],
        compiler_params=params(VMEM_BYTES),
        name="tile_sums_second",
    )(columns, ensemble, state, climate, weight, *sums)


def matrix_kernel(masks, paired, myself_ref, near_ref, dest_ref, local_ref, conv_ref, matrix_ref):
    blocks, neigh, size, _ = conv_ref.shape
    nodes = blocks * size
    rows = [
        jnp.concatenate([conv_ref[b, k] for k in range(neigh)], axis=1) for b in range(blocks)
    ]
    if paired:
        numbers = near_ref[near_ref.shape[0] - EXTRA :, :].astype(FULL).astype(jnp.int32)
        near = {
            (b, k): jnp.broadcast_to(numbers[b : b + 1, k : k + 1], (1, nodes))
            for b in range(blocks)
            for k in range(neigh)
        }
    else:
        near = {(b, k): near_ref[b, k] for b in range(blocks) for k in range(neigh)}
    row = lax.broadcasted_iota(jnp.int32, (size, nodes), 0)
    for s in range(dest_ref.shape[1] // nodes):
        source = slot_source(masks, myself_ref[0], s)
        span = pl.ds(pl.multiple_of(source * nodes, nodes), nodes)
        tile_node = dest_ref[:, span] * nodes + local_ref[:, span]
        for b in range(blocks):
            place = jnp.concatenate(
                [ones_where(row == tile_node - near[b, k] * size) for k in range(neigh)], axis=0
            )
            block = jnp.dot(rows[b], place, preferred_element_type=FULL)
            matrix_ref[s * nodes : (s + 1) * nodes, b * size : (b + 1) * size] = block.T.astype(HALF)


def run_matrix(myself, near, dest, local, conv_blocks, paired):
    blocks, _, size, _ = conv_blocks.shape
    scalars = pl.BlockSpec(memory_space=pltpu.SMEM)
    return pl.pallas_call(
        functools.partial(matrix_kernel, tile_masks(), paired),
        in_specs=[scalars, whole(1)[0] if paired else scalars] + whole(3),
        out_specs=whole(1)[0],
        out_shape=jax.ShapeDtypeStruct((dest.shape[1], blocks * size), HALF),
        compiler_params=params(TABLE_BYTES),
        name="pair_matrix" if paired else "node_matrix",
    )(myself, near, dest, local, conv_blocks)


def select_kernel(masks, nodes, myself_ref, dest_ref, local_ref, select_ref):
    span = pl.ds(pl.multiple_of(myself_ref[0] * nodes, nodes), nodes)
    dest, local = (
        jnp.concatenate([ref[k : k + 1, span] for k in range(2)], axis=1)
        for ref in (dest_ref, local_ref)
    )
    row = lax.broadcasted_iota(jnp.int32, (nodes, 2 * nodes), 0)
    for s in range(dest_ref.shape[1] // nodes):
        source = slot_source(masks, myself_ref[0], s)
        select_ref[s * nodes : (s + 1) * nodes, :] = ones_where(
            row == jnp.where(dest == source, local, -1)
        )


def run_select(myself, dest, local, nodes):
    return pl.pallas_call(
        functools.partial(select_kernel, node_masks(), nodes),
        in_specs=[pl.BlockSpec(memory_space=pltpu.SMEM)] + whole(2),
        out_specs=whole(1)[0],
        out_shape=jax.ShapeDtypeStruct((dest.shape[1], 2 * nodes), HALF),
        compiler_params=params(TABLE_BYTES),
        name="selection",
    )(myself, dest, local)


def slot_product(feature, piece_refs, matrix_ref):
    span = piece_refs[0].shape[1]
    total = jnp.zeros((feature, matrix_ref.shape[1]), FULL)
    for s, piece in enumerate(piece_refs):
        total = total + jnp.dot(
            piece[0:feature, :],
            matrix_ref[s * span : (s + 1) * span, :],
            preferred_element_type=FULL,
        )
    return total


def nodes_kernel(near_ref, matrix_ref, *refs):
    piece_refs, out_ref = refs[:-1], refs[-1]
    feature = piece_refs[0].shape[0]
    out_ref[0:feature, :] = slot_product(feature, piece_refs, matrix_ref).astype(HALF)
    blocks, neigh = near_ref.shape
    extra = (EXTRA, out_ref.shape[1])
    row = lax.broadcasted_iota(jnp.int32, extra, 0)
    lane = lax.broadcasted_iota(jnp.int32, extra, 1)
    numbers = jnp.zeros(extra, jnp.int32)
    for b in range(blocks):
        for k in range(neigh):
            numbers = jnp.where((row == b) & (lane == k), near_ref[b, k], numbers)
    out_ref[feature:, :] = numbers.astype(FULL).astype(HALF)


def run_nodes(neighbours, matrix, partial_all):
    feature = partial_all[0].shape[0]
    return pl.pallas_call(
        nodes_kernel,
        in_specs=[pl.BlockSpec(memory_space=pltpu.SMEM)] + whole(1 + len(partial_all)),
        out_specs=whole(1)[0],
        out_shape=jax.ShapeDtypeStruct((feature + EXTRA, matrix.shape[1]), HALF),
        compiler_params=params(TABLE_BYTES),
        name="nodes",
    )(neighbours, matrix, *partial_all)


def pair_nodes_kernel(count, *refs):
    matrix_refs, piece_refs, out_ref = refs[:count], refs[count:-1], refs[-1]
    width = matrix_refs[0].shape[1]
    for i, matrix_ref in enumerate(matrix_refs):
        out_ref[:, i * width : (i + 1) * width] = slot_product(
            out_ref.shape[0], piece_refs, matrix_ref
        ).astype(HALF)


def run_pair_nodes(matrices, partial_all):
    feature = partial_all[0].shape[0]
    return pl.pallas_call(
        functools.partial(pair_nodes_kernel, len(matrices)),
        in_specs=whole(len(matrices) + len(partial_all)),
        out_specs=whole(1)[0],
        out_shape=jax.ShapeDtypeStruct((feature, sum(m.shape[1] for m in matrices)), HALF),
        compiler_params=params(TABLE_BYTES),
        name="pair_nodes",
    )(*matrices, *partial_all)


def expansion_kernel(width, weight_ref, expand_ref, columns_ref):
    columns_ref[...] = tile_columns(width)
    inside = tile_indicator(width // TILE, width)

    def step(i, carry):
        weight = weight_ref[:, pl.ds(pl.multiple_of(i * width, width), width)]
        high = weight.astype(HALF).astype(FULL)
        low = weight - high
        expand_ref[i] = jnp.concatenate(
            [
                jnp.where(inside, source[k : k + 1, :], 0.0).astype(HALF)
                for source in (high, low)
                for k in range(2)
            ],
            axis=0,
        )
        return carry

    lax.fori_loop(0, expand_ref.shape[0], step, 0)


def run_expansion(width, interp_weight):
    return pl.pallas_call(
        functools.partial(expansion_kernel, width),
        in_specs=whole(1),
        out_specs=whole(2),
        out_shape=[
            jax.ShapeDtypeStruct((interp_weight.shape[1] // width, 4 * width // TILE, width), HALF),
            jax.ShapeDtypeStruct((width, width // TILE), HALF),
        ],
        compiler_params=params(TABLE_BYTES),
        name="expansion",
    )(interp_weight)


def spread_kernel(slots, ensemble_ref, select_ref, expand_ref, *refs):
    node_refs, out_refs, values_ref = refs[:slots], refs[slots : slots + 2], refs[slots + 2]
    members, levels, _ = ensemble_ref.shape
    steps, _, width = expand_ref.shape
    tiles = width // TILE
    feature = members * levels
    pairs = select_ref.shape[1]
    values = slot_product(feature, node_refs, select_ref)
    lane = lax.broadcasted_iota(jnp.int32, (feature, LANES), 1)
    group = LANES // tiles
    for i in range(steps):
        first = i // group * LANES
        ends = [values[:, k * pairs // 2 + first : k * pairs // 2 + first + LANES] for k in range(2)]
        left = ends[0]
        for place in range(group):
            shift = (place - i % group) * tiles % LANES
            moved = ends[place % 2] if shift == 0 else pltpu.roll(ends[place % 2], shift, 1)
            left = moved if place == 0 else jnp.where(lane < place * tiles, left, moved)
        values_ref[i] = left.astype(HALF)
    piece = 2 * LANES

    half = steps // 2
    for i in range(steps):
        for c in range(0, width, piece):
            field = jnp.dot(
                values_ref[i], expand_ref[i, :, c : c + piece], preferred_element_type=FULL
            )
            field = field.reshape(members, levels, piece)
            start = i * width + c
            terms = ensemble_ref[:, :, start : start + piece].astype(FULL) * field
            start = i % half * width + c
            out_refs[i // half][:, start : start + piece] = jnp.sum(terms, axis=0).astype(HALF)


def run_spread(select, ensemble, expand, nodes_all):
    members, levels, fine, _, steps = column_sizes(ensemble)
    slots = len(nodes_all)
    return pl.pallas_call(
        functools.partial(spread_kernel, slots),
        in_specs=whole(3 + slots),
        out_specs=whole(2),
        out_shape=[jax.ShapeDtypeStruct((levels, fine // 2), HALF)] * 2,
        scratch_shapes=[pltpu.VMEM((steps, members * levels, LANES), HALF)],
        compiler_params=params(VMEM_BYTES),
        name="spread",
    )(ensemble, select, expand, *nodes_all)


def add_half(one, two):
    return (one.astype(FULL) + two.astype(FULL)).astype(HALF)


def member_sum(halves):
    size = lax.axis_size("mem")
    masks = [1 << i for i in range(size.bit_length() - 1)]
    orders = [masks, masks[::-1]]
    for step in range(len(masks) - 1):
        moved = [swap(part, "mem", order[step]) for part, order in zip(halves, orders)]
        halves = [add_half(part, other) for part, other in zip(halves, moved)]
    moved = [swap(part, "mem", order[-1]) for part, order in zip(halves, orders)]
    return halves[0], moved[0], halves[1], moved[1]


def per_device(
    increment,
    ensemble,
    climate,
    restrict_dest,
    restrict_local,
    restrict_weight,
    conv_blocks,
    neighbours,
    interp_dest,
    interp_local,
    interp_weight,
):
    myself = lax.axis_index("col")[None]
    members = ensemble.shape[0]
    nodes = ensemble.shape[2] // TILE
    scale = 1.0 / (members * lax.axis_size("mem") - 1)
    weight = restrict_weight[None, :]

    tables = [restrict_dest.reshape(1, -1), restrict_local.reshape(1, -1)]

    partial_all = gather_tiles(run_first(increment, weight, ensemble))
    matrix = run_matrix(myself, neighbours, *tables, conv_blocks, False)
    select = run_select(myself, interp_dest.T, interp_local.T, nodes)
    expand, columns = run_expansion(column_sizes(ensemble)[3], interp_weight)

    nodes_all = gather_nodes(run_nodes(neighbours, matrix, partial_all))
    sums = member_sum(run_spread(select, ensemble, expand, nodes_all))
    once_applied, partial = run_second(scale, columns, increment, climate, sums, weight, ensemble)
    partial_all = gather_tiles(partial)
    if is_paired():
        carrier = nodes_all[node_masks().index(PAIR)]
        conv_pair = swap(conv_blocks, "col", PAIR)
        matrices = [matrix, run_matrix(myself, carrier, *tables, conv_pair, True)]
        nodes_all = gather_pairs(run_pair_nodes(matrices, partial_all))
    else:
        nodes_all = gather_nodes(run_pair_nodes([matrix], partial_all))
    sums = member_sum(run_spread(select, ensemble, expand, nodes_all))
    total = jnp.concatenate(
        [sums[2 * i].astype(FULL) + sums[2 * i + 1].astype(FULL) for i in range(2)], axis=1
    )
    return once_applied, climate * once_applied + total * scale


def solution(mesh):
    in_specs = (
        P(None, "col"),
        P("mem", None, "col"),
        P(None, "col"),
        P(),
        P(),
        P("col"),
        P("col", None, None, None),
        P("col", None),
        P(),
        P(),
        P(None, "col"),
    )
    out_specs = (P(None, "col"), P(None, "col"))

    return jax.shard_map(per_device, mesh=mesh, in_specs=in_specs, out_specs=out_specs, check_vma=False)
```
